256 devices in a mesh: grp: 8 (over z_lo, y), mem: 32 (over x, z_hi, core).
Axes of the slice: x: 4, y: 4, z: 8 (z_hi: 4, z_lo: 2; z = z_hi * 2 + z_lo), core: 2. Of those that a mesh axis runs over, the one named last changes fastest.
Arguments:
- pooled: bfloat16 [32768, 5120], P(('grp', 'mem')), may hold values from -24 to 24
- grad_hidden: bfloat16 [32768, 512], P(('grp', 'mem')), may hold values from -0.059814453 to 0.059814453
- w_first: bfloat16 [5120, 512], replicated, may hold values from -0.078125 to 0.078125
- bias_first: float32 [512], replicated, may hold values from -4 to 4
- table_owner: int32 [8, 32], P('grp'), may hold values from 0 to 31, each once within a row
- shard_owner: int32 [8, 32], P('grp'), may hold values from 0 to 31, each once within a row
- lookups_whole: int32 [8, 32, 4096, 8], P('grp', 'mem'), may hold values from 0 to 1023
- lookups_split: int32 [8, 8, 4096, 8], P('grp'), may hold values from 0 to 1023
- table_whole: float32 [8, 32, 128, 1024], P('grp', 'mem'), may hold values from -3 to 3
- accum_whole: float32 [8, 32, 1024], P('grp', 'mem'), may hold values from 2e-05 to 0.0002
- table_split: float32 [8, 32, 32, 1024], P('grp', 'mem'), may hold values from -3 to 3
- accum_split: float32 [8, 8, 1024], P('grp'), may hold values from 2e-05 to 0.0002
Outputs:
- grad_first: float32 [5120, 512], P('mem')
- grad_bias: float32 [512], replicated
- new_whole: float32 [8, 32, 128, 1024], P('grp', 'mem')
- new_split: float32 [8, 32, 32, 1024], P('grp', 'mem')
The draws below stay inside these ranges and needn't reach their ends.
Inputs may be any that keep to these rules, and one draw needn't show every extreme that they name: `table_owner`: each row is a permutation of the owner slots. `shard_owner`: each row is a permutation of the owner slots.
All inputs are finite; a program needn't handle non-finite values.
Results may differ from the reference program's by a relative error of at most 0.0055.
Values may be sent and summed in bfloat16 or wider, within the bound.
A program may use at most 128 MiB of HBM per device.

```python
import math
import jax
import jax.numpy as jnp
from jax import lax

E = 128
H = 512
CS = 4
POOL = 8
ROWS = 1024
ROWS_C = 1024
SAMPLES = 4096
SAMPLES_ALL = 32768
NT = 32
NC = 8
COLS = 32
FEATS = 5120
N_GRP = 8
N_MEM = 32


def touch_ends(result, own_key, least, largest):
    longest = result.shape.index(max(result.shape))
    spots = []
    for shift in (0, 1):
        where = [jax.random.randint(jax.random.fold_in(own_key, axis), (), 0, length) for axis, length in enumerate(result.shape)]
        where[longest] = (where[longest] + shift) % result.shape[longest]
        spots.append(tuple(where))
    return result.at[spots[0]].set(least).at[spots[1]].set(largest)


def raised(values, own_key, source, target, shards_of, factor):
    def block_of(position):
        return (jnp.arange(values.shape[position]) // (values.shape[position] // shards_of)).reshape((-1,) + (1,) * (values.ndim - 1 - position))

    one_side = jax.random.permutation(own_key, shards_of)[block_of(target)]
    second = (block_of(target) + shards_of // 2) % shards_of
    return jnp.where((block_of(source) == one_side) | (block_of(source) == second), factor * values, values)


def block_scale(key, extent, split, low, high):
    gain, own = 1.0, jax.random.fold_in(key, 6)
    for axis_at, blocks in split:
        steps = jnp.exp(jax.random.uniform(jax.random.fold_in(own, axis_at), (blocks,), jnp.float32, low / len(split), high / len(split)))
        gain = gain * jnp.repeat(steps, extent[axis_at] // blocks).reshape([-1 if axis == axis_at else 1 for axis in range(len(extent))])
    return gain


def gaussian(rng, extent, scale, bound, shards=(), kind=jnp.bfloat16):
    result = jax.random.normal(rng, extent, jnp.float32) * scale
    if len(shards) > 0:
        result = block_scale(rng, extent, shards, -0.22, 0.18) * result
    return jnp.clip(result, min=-bound, max=bound).astype(kind)


def gaussian_with(rng, dims, deviation, limit, pieces, heavy, kind=jnp.bfloat16):
    drawn = deviation * jax.random.normal(rng, dims, jnp.float32)
    if pieces:
        drawn = drawn * block_scale(rng, dims, pieces, -0.22, 0.18)
    return jnp.clip(raised(drawn, jax.random.fold_in(rng, 3), *heavy), -limit, limit).astype(kind)


def setup_inputs(seed: int = 0) -> dict:
    streams_of = jax.random.split(jax.random.key(seed), 13)
    pooled = gaussian_with(streams_of[0], (SAMPLES_ALL, FEATS), 1.0, 24.0, ((0, 256),), (0, 1, 256, 6.0))
    grad_hidden = gaussian(streams_of[1], (SAMPLES_ALL, H), 0.01, 0.059814453, ((0, 256),))
    w_first = gaussian(streams_of[2], (FEATS, H), FEATS ** -0.5, 0.078125)
    bias_first = gaussian(streams_of[3], (H,), 1.0, 4.0, (), jnp.float32)
    table_owner = jax.vmap(lambda own: jax.random.permutation(own, NT))(jax.random.split(streams_of[4], N_GRP)).reshape((N_GRP, NT)).astype(jnp.int32)
    shard_owner = jax.vmap(lambda own: jax.random.permutation(own, N_MEM))(jax.random.split(streams_of[5], N_GRP)).reshape((N_GRP, N_MEM)).astype(jnp.int32)
    lookups_whole = touch_ends(jax.random.randint(streams_of[6], (N_GRP, N_MEM, SAMPLES, POOL), 0, ROWS), jax.random.fold_in(streams_of[6], 1), 0, ROWS - 1).astype(jnp.int32)
    lookups_split = touch_ends(jax.random.randint(streams_of[7], (N_GRP, NC, SAMPLES, POOL), 0, ROWS_C), jax.random.fold_in(streams_of[7], 1), 0, ROWS_C - 1).astype(jnp.int32)
    table_whole = gaussian(streams_of[8], (N_GRP, N_MEM, E, ROWS), 0.5, 3.0, ((0, 8), (1, 32)), jnp.float32)
    accum_whole = jnp.clip(jnp.exp(math.log(0.0002) - 2.3025851 * jax.random.uniform(streams_of[9], (N_GRP, N_MEM, ROWS), jnp.float32) ** block_scale(streams_of[9], (N_GRP, N_MEM, ROWS), ((0, 8), (1, 32)), -0.2, 0.2)), 1.9999999494757503e-05, 0.0002)
    table_split = gaussian(streams_of[10], (N_GRP, N_MEM, COLS, ROWS_C), 0.5, 3.0, ((0, 8), (1, 32)), jnp.float32)
    accum_split = jnp.clip(jnp.exp(math.log(0.0002) - 2.3025851 * jax.random.uniform(streams_of[11], (N_GRP, NC, ROWS_C), jnp.float32) ** block_scale(streams_of[11], (N_GRP, NC, ROWS_C), ((0, 8),), -0.2, 0.2)), 1.9999999494757503e-05, 0.0002)
    return {"pooled": pooled, "grad_hidden": grad_hidden, "w_first": w_first, "bias_first": bias_first, "table_owner": table_owner, "shard_owner": shard_owner, "lookups_whole": lookups_whole, "lookups_split": lookups_split, "table_whole": table_whole, "accum_whole": accum_whole, "table_split": table_split, "accum_split": accum_split}


LEARN_RATE = 0.5
EPSILON = 1e-08

def row_sums(values, key_rows, row_count):
    pool_size = key_rows.shape[1]
    spread = jnp.repeat(values.astype(jnp.float32), pool_size, axis=0)
    flat_keys = key_rows.reshape(-1).astype(jnp.int32)
    return jax.ops.segment_sum(spread, flat_keys, num_segments=row_count).T

def adagrad(weights_in, accum_rows, row_grad, squares):
    state_rows = accum_rows + squares / E
    return weights_in - LEARN_RATE * row_grad / (jnp.sqrt(state_rows) + EPSILON)

def whole_slot(entries):
    values, key_rows, weights_in, accum_rows = entries
    row_grad = row_sums(values, key_rows, ROWS)
    return adagrad(weights_in, accum_rows, row_grad, lax.optimization_barrier(jnp.sum(row_grad * row_grad, axis=0)))

def split_slot(entries):
    return row_sums(entries[0], entries[1], ROWS_C)

def group_update(entries):
    back_rows, owner_row, shard_row, keys_whole, keys_split, table_whole, accum_whole, table_split, accum_split = entries
    whole_order = jnp.argsort(owner_row).astype(jnp.int32)
    split_order = jnp.argsort(shard_row).astype(jnp.int32)
    whole_part = back_rows[:, :N_MEM * E].reshape(SAMPLES, N_MEM, E)
    split_part = back_rows[:, N_MEM * E:].reshape(SAMPLES, N_MEM, COLS)
    whole_part = jnp.transpose(jnp.take(whole_part, whole_order, axis=1), (1, 0, 2))
    split_part = jnp.transpose(jnp.take(split_part, split_order, axis=1), (1, 0, 2))
    new_whole = lax.map(whole_slot, (whole_part, keys_whole, table_whole, accum_whole))
    owned_table = (split_order // CS).astype(jnp.int32)
    split_grads = lax.map(split_slot, (split_part, keys_split[owned_table]))
    squares = lax.optimization_barrier(jnp.sum(split_grads * split_grads, axis=1))
    table_squares = jax.ops.segment_sum(squares, owned_table, num_segments=NC)
    totals = table_squares[owned_table]
    new_split = adagrad(table_split, accum_split[owned_table][:, None, :], split_grads, totals[:, None, :])
    return (new_whole, new_split)

def reference(pooled, grad_hidden, w_first, bias_first, table_owner, shard_owner, lookups_whole, lookups_split, table_whole, accum_whole, table_split, accum_split):
    pre_act = jnp.dot(pooled, w_first, preferred_element_type=jnp.float32) + bias_first
    sigmoid_pre = jax.nn.sigmoid(pre_act)
    gradient_slope = sigmoid_pre * (1.0 + pre_act * (1.0 - sigmoid_pre))
    delta_rows = (grad_hidden.astype(jnp.float32) * gradient_slope).astype(jnp.bfloat16)
    back_rows = jnp.dot(delta_rows, w_first.T, preferred_element_type=jnp.float32).astype(jnp.bfloat16)
    grad_first = jnp.dot(pooled.T, delta_rows, preferred_element_type=jnp.float32)
    grad_bias = lax.optimization_barrier(jnp.sum(delta_rows.astype(jnp.float32), axis=0))
    new_whole, new_split = lax.map(group_update, (back_rows.reshape(N_GRP, SAMPLES, FEATS), table_owner, shard_owner, lookups_whole, lookups_split, table_whole, accum_whole, table_split, accum_split))
    return (grad_first, grad_bias, new_whole, new_split)
```

```python
import jax
import jax.numpy as jnp
from jax import lax
from jax.experimental import pallas as pl
from jax.experimental.pallas import tpu as pltpu
from jax.sharding import Mesh
from jax.sharding import PartitionSpec as P

E = 128
CS = 4
COLS = 32
ZL, Y, X, ZH, C = "grp_0", "grp_1", "mem_0", "mem_1", "mem_2"
SIZE = {ZL: 2, Y: 4, X: 4, ZH: 4, C: 2}
MEM = (X, ZH, C)
GRP = (ZL, Y)
GRP_MEM = GRP + MEM
LEARN_RATE = 0.5
EPSILON = 1e-08
MESH = pl.DeviceIdType.MESH
BF = jnp.bfloat16
F32 = jnp.float32


def remote(src, dst, ssem, rsem, dev):
    return pltpu.make_async_remote_copy(
        src_ref=src, dst_ref=dst, send_sem=ssem, recv_sem=rsem, device_id=dev, device_id_type=MESH
    )


def kernel(
    owner_ref, sowner_ref, pooled_ref, gh_ref, w_hbm, bias_ref, lkw_ref, lks_ref,
    tw_ref, aw_ref, ts_ref, as_ref,
    gf_ref, gb_ref, nw_ref, ns_ref,
    w_v, pt, pr, gbuf, pp, yr, zs, zr, bs, br, cw, cs, accw, accs, bacc, wtct, pre, keys_c, gr,
    w_sem, own_sem, sp, rp, sa, sb, sc, rg, sy, ry, sz, rz, sg, rgf, sbi, rbi,
):
    x, zh, c = lax.axis_index(X), lax.axis_index(ZH), lax.axis_index(C)
    y, zl = lax.axis_index(Y), lax.axis_index(ZL)

    def off(axis, d):
        return lax.rem(lax.axis_index(axis) + d, SIZE[axis])

    load_w = pltpu.make_async_copy(w_hbm, w_v, w_sem)
    load_w.start()

    barrier = pltpu.get_barrier_semaphore()
    peers = []
    for d in (1, 2, 3):
        peers.append({X: off(X, d)})
        peers.append({X: off(X, d), C: 1 - c})
        peers.append({ZH: off(ZH, d)})
        peers.append({ZH: off(ZH, d), ZL: 1 - zl})
        peers.append({Y: off(Y, d)})
        peers.append({Y: off(Y, d), ZL: 1 - zl})
    peers.append({C: 1 - c})
    peers.append({ZL: 1 - zl})
    for p in peers:
        pl.semaphore_signal(barrier, inc=1, device_id=p, device_id_type=MESH)
    pl.semaphore_wait(barrier, len(peers))

    for t in range(40):
        tile = pooled_ref[:, 128 * t : 128 * t + 128].T
        done = 0
        while done < 128:
            f = 128 * t + done
            m, r = f // 160, f % 160
            n = min(160 - r, 128 - done)
            pt[(m // 8), m % 2, (m // 2) % 4, r : r + n, :] = tile[done : done + n, :]
            done += n

    def piece(dx, dc):
        xd, cd = off(X, dx), off(C, dc)
        i = dx * 2 + dc
        return remote(pt.at[xd, cd], pr.at[x * 2 + c], sp.at[i], rp.at[x * 2 + c], {X: xd, C: cd})

    def piece_in(xs, csrc):
        return remote(pt.at[0, 0], pr.at[xs * 2 + csrc], sp.at[0], rp.at[xs * 2 + csrc], {C: 1 - c})

    own_piece = pltpu.make_async_copy(pt.at[x, c], pr.at[x * 2 + c], own_sem)
    own_piece.start()
    piece(0, 1).start()
    piece(1, 0).start()
    piece(3, 0).start()

    load_w.wait()
    pre[...] = jnp.zeros_like(pre)

    @pl.loop(0, 8)
    def _(k):
        cols = pl.ds(pl.multiple_of(k * 640, 640), 640)
        wk = w_v[pl.ds(k * 5, 5)].reshape(640, 512)
        pre[...] += jnp.dot(pooled_ref[:, cols], wk, preferred_element_type=F32)

    pre_act = pre[...] + bias_ref[...]
    sg_ = jax.nn.sigmoid(pre_act)
    slope = sg_ * (1.0 + pre_act * (1.0 - sg_))
    my_rows = pl.ds(pl.multiple_of(c * 128, 128), 128)
    gbuf[x * 4 + zh, my_rows, :] = (gh_ref[...].astype(F32) * slope).astype(BF)

    def half(h, a, b, cc):
        rows = pl.ds(pl.multiple_of(cc * 128 + h * 64, 64), 64)
        return gbuf.at[a * 4 + b, rows, :]

    def slot(h, a, b, cc):
        return rg.at[h, a * 8 + b * 2 + cc]

    def first_hop(h, d):
        ref = half(h, x, zh, c)
        dev = {ZH: off(ZH, d)} if h == 0 else {X: off(X, d)}
        return remote(ref, ref, sa.at[h, d - 1], slot(h, x, zh, c), dev)

    def second_hop(h, e, d):
        a, b = (x, off(ZH, e)) if h == 0 else (off(X, e), zh)
        ref = half(h, a, b, c)
        dev = {X: off(X, d)} if h == 0 else {ZH: off(ZH, d)}
        return remote(ref, ref, sb.at[h, e * 3 + d - 1], slot(h, a, b, c), dev)

    def to_core(h, da, db):
        a, b = off(X, da), off(ZH, db)
        ref = half(h, a, b, c)
        return remote(ref, ref, sc.at[h, da * 4 + db], slot(h, a, b, c), {C: 1 - c})

    def arrive(h, da, db, dc):
        a, b, cc = off(X, da), off(ZH, db), off(C, dc)
        ref = half(h, a, b, cc)
        remote(ref, ref, sa.at[0, 0], slot(h, a, b, cc), {C: 1 - c}).wait_recv()

    for h in (1, 0):
        for d in (1, 3, 2):
            first_hop(h, d).start()
    for h in (0, 1):
        for d in (1, 3, 2):
            second_hop(h, 0, d).start()
    for h in (0, 1):
        to_core(h, 0, 0).start()
    piece(1, 1).start()
    piece(3, 1).start()
    piece(2, 0).start()
    piece(2, 1).start()

    me = x * 8 + zh * 2 + c

    def find(ref, label):
        return lax.fori_loop(0, 32, lambda i, at: jnp.where(ref[0, i] == me, label(i), at), 0)

    whole_t = find(owner_ref, lambda i: i)
    split_t = find(sowner_ref, lambda i: 32 + i // CS)
    split_c = find(sowner_ref, lambda i: i // CS)
    quarter = find(sowner_ref, lambda i: lax.rem(i, CS))
    wtct[:, :128] = w_v[whole_t].T
    wtct[:, 128:] = w_v[split_t].T
    keys_c[...] = lks_ref[split_c]

    def count_block(keys, out, cols):
        lo = jnp.bitwise_and(keys, 127)
        field = jnp.left_shift(1, jnp.right_shift(keys, 7) * 4)
        sub = lax.broadcasted_iota(jnp.int32, (128, 128), 0)
        packed = jnp.zeros((128, 128), jnp.int32)
        for p in range(8):
            packed += jnp.where(lo[p : p + 1, :] == sub, field[p : p + 1, :], 0)
        for h in range(8):
            n = jnp.bitwise_and(jnp.right_shift(packed, 4 * h), 15)
            out[h * 128 : h * 128 + 128, cols] = n.astype(F32).astype(BF)

    def count(k, carry=None):
        cols = pl.ds(pl.multiple_of(k * 128, 128), 128)
        count_block(lkw_ref[:, cols], cw, cols)
        count_block(keys_c[:, cols], cs, cols)

    @pl.loop(0, 3)
    def _(j):
        e = 1 + lax.rem(2 * j, 3)
        for h in (1, 0):
            da, db = (0, e) if h == 0 else (e, 0)
            pl.loop(j * 10 + (1 - h) * 5, j * 10 + (1 - h) * 5 + 5)(lambda k: count(k))
            arrive(h, da, db, 0)
            for d in (1, 3, 2):
                second_hop(h, e, d).start()
            to_core(h, da, db).start()

    pl.loop(30, 32)(lambda k: count(k))

    for d in (1, 3, 2):
        arrive(0, d, 0, 0)
        to_core(0, d, 0).start()
    own_piece.wait()
    for i in range(1, 8):
        piece_in(off(X, i // 2), off(C, i % 2)).wait_recv()
    for d in range(4):
        for h in (0, 1):
            arrive(h, d, 0, 1)

    @pl.loop(0, 4)
    def _(q):
        total = jnp.zeros((160, 512), F32)
        for xs in range(4):
            both = jnp.concatenate([pr[2 * xs, q], pr[2 * xs + 1, q]], axis=1)
            total += jnp.dot(both, gbuf[xs * 4 + zh], preferred_element_type=F32)
        low = total.astype(BF)
        for j in range(4):
            pp[j, q] = low[:, 128 * j : 128 * j + 128]

    def along_y(d):
        yd = off(Y, d)
        return remote(pp.at[yd], yr.at[y], sy.at[d - 1], ry.at[y], {Y: yd})

    def from_y(d):
        ys = off(Y, d)
        return remote(pp.at[ys], yr.at[ys], sy.at[0], ry.at[ys], {Y: ys})

    for d in (1, 3, 2):
        along_y(d).start()

    accw[...] = jnp.zeros_like(accw)
    accs[...] = jnp.zeros_like(accs)
    bacc[...] = jnp.zeros_like(bacc)

    def tables(da, db):
        cb = off(X, da) * 4 + off(ZH, db)
        rows = gbuf[cb]
        cols = pl.ds(pl.multiple_of(cb * 256, 256), 256)
        back = jnp.dot(rows, wtct[...], preferred_element_type=F32).astype(BF)
        accw[...] += jnp.dot(cw[:, cols], back[:, :128], preferred_element_type=F32)
        accs[...] += jnp.dot(cs[:, cols], back[:, 128:], preferred_element_type=F32)
        bacc[...] += jnp.dot(jnp.ones((8, 256), BF), rows, preferred_element_type=F32)

    tables(0, 0)

    for b in (1, 3, 2):
        arrive(1, 0, b, 0)
        to_core(1, 0, b).start()
        tables(b, 0)

    for d in (1, 3, 2):
        from_y(d).wait_recv()

    @pl.loop(0, 4)
    def _(q):
        total = pp[y, q].astype(F32)
        for d in (1, 2, 3):
            total += yr[off(Y, d), q].astype(F32)
        zs[q * 2] = total[:80].astype(BF)
        zs[q * 2 + 1] = total[80:].astype(BF)

    zme = zh * 2 + zl
    others = [(1, 0), (3, 0), (0, 1), (1, 1), (3, 1), (2, 0), (2, 1)]

    def along_z(i):
        zd, ld = off(ZH, others[i][0]), off(ZL, others[i][1])
        return remote(zs.at[zd * 2 + ld], zr.at[zme], sz.at[i], rz.at[zme], {ZH: zd, ZL: ld})

    def from_z(i):
        s = off(ZH, others[i][0]) * 2 + off(ZL, others[i][1])
        return remote(zs.at[s], zr.at[s], sz.at[0], rz.at[s], {C: 1 - c})

    for i in range(7):
        along_z(i).start()

    for b in (1, 3, 2):
        arrive(0, 0, b, 1)
        arrive(1, 0, b, 1)
        tables(0, b)

    def far(k):
        return (1, 3, 2)[k // 3], (1, 3, 2)[k % 3]

    def relay(k):
        da, db = far(k)
        for h in (0, 1):
            arrive(h, da, db, 0)
            to_core(h, da, db).start()

    def far_tables(k):
        da, db = far(k)
        arrive(0, da, db, 1)
        arrive(1, da, db, 1)
        tables(da, db)

    relay(0)

    for k in range(4):
        relay(k + 1)
        far_tables(k)

    for i in range(7):
        from_z(i).wait_recv()
    total = zs[zme].astype(F32)
    for i in range(7):
        total += zr[off(ZH, others[i][0]) * 2 + off(ZL, others[i][1])].astype(F32)

    gme = y * 2 + zl
    gr[gme] = total
    group = [(1, 0), (3, 0), (0, 1), (1, 1), (3, 1), (2, 0), (2, 1)]

    def give(i):
        yd, ld = off(Y, group[i][0]), off(ZL, group[i][1])
        return remote(gr.at[gme], gr.at[gme], sg.at[i], rgf.at[gme], {Y: yd, ZL: ld})

    def take(i):
        g = off(Y, group[i][0]) * 2 + off(ZL, group[i][1])
        return remote(gr.at[g], gr.at[g], sg.at[0], rgf.at[g], {C: 1 - c})

    for i in range(7):
        give(i).start()

    for k in range(4, 8):
        relay(k + 1)
        far_tables(k)

    far_tables(8)

    bs[...] = bacc[...]

    def give_bias(i):
        yd, ld = off(Y, group[i][0]), off(ZL, group[i][1])
        return remote(bs, br.at[y * 2 + zl], sbi.at[i], rbi.at[y * 2 + zl], {Y: yd, ZL: ld})

    def take_bias(i):
        s = off(Y, group[i][0]) * 2 + off(ZL, group[i][1])
        return remote(bs, br.at[s], sbi.at[0], rbi.at[s], {C: 1 - c})

    for i in range(7):
        give_bias(i).start()

    grad = accw[...].T
    square = jnp.sum(grad * grad, axis=0, keepdims=True)
    scale = LEARN_RATE / (jnp.sqrt(aw_ref[...] + square / E) + EPSILON)
    nw_ref[...] = tw_ref[...] - grad * scale
    grads = accs[...].T
    squares = jnp.sum(grads * grads, axis=0, keepdims=True)
    tab = lax.broadcasted_iota(jnp.int32, (8, 1024), 0)
    state = jnp.sum(jnp.where(tab == split_c, as_ref[...], 0.0), axis=0, keepdims=True)
    scales = LEARN_RATE / (jnp.sqrt(state + squares / E) + EPSILON)
    mine = grads[:COLS]
    for q in range(1, CS):
        mine = jnp.where(quarter == q, grads[q * COLS : (q + 1) * COLS], mine)
    ns_ref[...] = ts_ref[...] - mine * scales

    for i in range(7):
        take_bias(i).wait_recv()
    bias_sum = bs[0:1, :]
    for i in range(7):
        s = off(Y, group[i][0]) * 2 + off(ZL, group[i][1])
        bias_sum += br[s, 0:1, :]
    gb_ref[...] = bias_sum

    for i in range(7):
        take(i).wait_recv()
    for yy in range(4):
        for ll in range(2):
            gf_ref[80 * ll : 80 * ll + 80, 128 * yy : 128 * yy + 128] = gr[yy * 2 + ll]
    for i in range(1, 8):
        piece(i // 2, i % 2).wait_send()
    for h in (0, 1):
        for d in (1, 2, 3):
            first_hop(h, d).wait_send()

        @pl.loop(0, 4)
        def _(e):
            for d in (1, 2, 3):
                second_hop(h, e, d).wait_send()

        @pl.loop(0, 16)
        def _(i):
            to_core(h, i // 4, lax.rem(i, 4)).wait_send()

    for d in (1, 2, 3):
        along_y(d).wait_send()
    for i in range(7):
        along_z(i).wait_send()
        give(i).wait_send()
        give_bias(i).wait_send()


VM = pl.BlockSpec(memory_space=pltpu.VMEM)
SM = pl.BlockSpec(memory_space=pltpu.SMEM)
ANY = pl.BlockSpec(memory_space=pl.ANY)
DMA = pltpu.SemaphoreType.DMA


def per_device(
    pooled, grad_hidden, w_first, bias_first, table_owner, shard_owner, lookups_whole,
    lookups_split, table_whole, accum_whole, table_split, accum_split,
):
    keys_whole = jnp.swapaxes(lookups_whole[0, 0], 0, 1)
    keys_split = jnp.swapaxes(lookups_split[0], 1, 2)
    outs = pl.pallas_call(
        kernel,
        out_shape=(
            jax.ShapeDtypeStruct((160, 512), F32),
            jax.ShapeDtypeStruct((1, 512), F32),
            jax.ShapeDtypeStruct((128, 1024), F32),
            jax.ShapeDtypeStruct((32, 1024), F32),
        ),
        in_specs=[SM, SM, VM, VM, ANY, VM, VM, VM, VM, VM, VM, VM],
        out_specs=(VM, VM, VM, VM),
        scratch_shapes=[
            pltpu.VMEM((40, 128, 512), BF),
            pltpu.VMEM((4, 2, 4, 160, 128), BF),
            pltpu.VMEM((8, 4, 160, 128), BF),
            pltpu.VMEM((16, 256, 512), BF),
            pltpu.VMEM((4, 4, 160, 128), BF),
            pltpu.VMEM((4, 4, 160, 128), BF),
            pltpu.VMEM((8, 80, 128), BF),
            pltpu.VMEM((8, 80, 128), BF),
            pltpu.VMEM((8, 512), F32),
            pltpu.VMEM((8, 8, 512), F32),
            pltpu.VMEM((1024, 4096), BF),
            pltpu.VMEM((1024, 4096), BF),
            pltpu.VMEM((1024, 128), F32),
            pltpu.VMEM((1024, 128), F32),
            pltpu.VMEM((8, 512), F32),
            pltpu.VMEM((512, 256), BF),
            pltpu.VMEM((128, 512), F32),
            pltpu.VMEM((8, 4096), jnp.int32),
            pltpu.VMEM((8, 80, 128), F32),
            DMA,
            DMA,
            DMA((8,)), DMA((8,)),
            DMA((2, 3)), DMA((2, 12)), DMA((2, 16)), DMA((2, 32)),
            DMA((3,)), DMA((4,)),
            DMA((7,)), DMA((8,)),
            DMA((7,)), DMA((8,)),
            DMA((7,)), DMA((8,)),
        ],
        compiler_params=pltpu.CompilerParams(
            collective_id=0, has_side_effects=True, vmem_limit_bytes=58 * 2**20
        ),
        name="step",
    )(
        table_owner, shard_owner, pooled, grad_hidden, w_first.reshape(40, 128, 512), bias_first[None], keys_whole,
        keys_split, table_whole[0, 0], accum_whole[0], table_split[0, 0], accum_split[0],
    )
    grad_first, grad_bias, new_whole, new_split = outs
    return grad_first, grad_bias[0], new_whole[None, None], new_split[None, None]


def solution(mesh):
    finer = Mesh(mesh.devices.reshape(2, 4, 4, 4, 2), GRP_MEM)
    in_specs = (
        P(GRP_MEM, None),
        P(GRP_MEM, None),
        P(),
        P(),
        P(GRP, None),
        P(GRP, None),
        P(GRP, MEM, None, None),
        P(GRP, None, None, None),
        P(GRP, MEM, None, None),
        P(GRP, MEM, None),
        P(GRP, MEM, None, None),
        P(GRP, None, None),
    )
    out_specs = (P(MEM, None), P(), P(GRP, MEM, None, None), P(GRP, MEM, None, None))
    return jax.shard_map(
        per_device, mesh=finer, in_specs=in_specs, out_specs=out_specs, check_vma=False
    )
```

```python
import jax
import jax.numpy as jnp
from jax import lax
from jax.experimental import pallas as pl
from jax.experimental.pallas import tpu as pltpu
from jax.sharding import Mesh
from jax.sharding import PartitionSpec as P

E = 128
CS = 4
COLS = 32
ZL, Y, X, ZH, C = "grp_0", "grp_1", "mem_0", "mem_1", "mem_2"
SIZE = {ZL: 2, Y: 4, X: 4, ZH: 4, C: 2}
MEM = (X, ZH, C)
GRP = (ZL, Y)
GRP_MEM = GRP + MEM
LEARN_RATE = 0.5
EPSILON = 1e-08
MESH = pl.DeviceIdType.MESH
BF = jnp.bfloat16
F32 = jnp.float32


def remote(src, dst, ssem, rsem, dev):
    return pltpu.make_async_remote_copy(
        src_ref=src, dst_ref=dst, send_sem=ssem, recv_sem=rsem, device_id=dev, device_id_type=MESH
    )


def kernel(
    owner_ref, sowner_ref, pooled_ref, gh_ref, w_hbm, bias_ref, lkw_ref, lks_hbm,
    gf_ref, gb_ref, accw, accs,
    w_v, lks_ref, pt, pr, gbuf, pp, yr, zs, zr, bs, by, bt, bz, cw, cs, wtct, pre, keys_c, gr,
    w_sem, lk_sem, own_sem, sp, rp, sa, sb, sc, rg, rh, sy, ry, sz, rz, sg, rgf, sby, rby, sbz, rbz,
):
    x, zh, c = lax.axis_index(X), lax.axis_index(ZH), lax.axis_index(C)
    y, zl = lax.axis_index(Y), lax.axis_index(ZL)

    def off(axis, d):
        return lax.rem(lax.axis_index(axis) + d, SIZE[axis])

    load_w = pltpu.make_async_copy(w_hbm, w_v, w_sem)
    load_w.start()
    load_keys = pltpu.make_async_copy(lks_hbm, lks_ref, lk_sem)
    load_keys.start()

    barrier = pltpu.get_barrier_semaphore()
    peers = []
    for d in (1, 2, 3):
        peers.append({X: off(X, d)})
        peers.append({X: off(X, d), C: 1 - c})
        peers.append({ZH: off(ZH, d)})
        peers.append({ZH: off(ZH, d), ZL: 1 - zl})
        peers.append({Y: off(Y, d)})
        peers.append({Y: off(Y, d), ZL: 1 - zl})
    peers.append({C: 1 - c})
    peers.append({ZL: 1 - zl})
    for p in peers:
        pl.semaphore_signal(barrier, inc=1, device_id=p, device_id_type=MESH)

    for t in range(40):
        tile = pooled_ref[:, 128 * t : 128 * t + 128].T
        done = 0
        while done < 128:
            f = 128 * t + done
            m, r = f // 160, f % 160
            n = min(160 - r, 128 - done)
            pt[(m // 8), m % 2, (m // 2) % 4, r : r + n, :] = tile[done : done + n, :]
            done += n

    def piece(dx, dc):
        xd, cd = off(X, dx), off(C, dc)
        i = dx * 2 + dc
        return remote(pt.at[xd, cd], pr.at[x * 2 + c], sp.at[i], rp.at[x * 2 + c], {X: xd, C: cd})

    def piece_in(xs, csrc):
        return remote(pt.at[0, 0], pr.at[xs * 2 + csrc], sp.at[0], rp.at[xs * 2 + csrc], {C: 1 - c})

    own_piece = pltpu.make_async_copy(pt.at[x, c], pr.at[x * 2 + c], own_sem)
    load_w.wait()
    pre[...] = jnp.zeros_like(pre)

    def tower(k):
        cols = pl.ds(pl.multiple_of(k * 640, 640), 640)
        wk = w_v[pl.ds(k * 5, 5)].reshape(640, 512)
        pre[...] += jnp.dot(pooled_ref[:, cols], wk, preferred_element_type=F32)

    pl.loop(0, 3)(tower)
    pl.semaphore_wait(barrier, len(peers))
    piece(1, 0).start()
    piece(3, 0).start()
    piece(0, 1).start()
    own_piece.start()
    pl.loop(3, 8)(tower)

    pre_act = pre[...] + bias_ref[...]
    sg_ = jax.nn.sigmoid(pre_act)
    slope = sg_ * (1.0 + pre_act * (1.0 - sg_))
    my_rows = pl.ds(pl.multiple_of(c * 128, 128), 128)
    gbuf[x * 4 + zh, my_rows, :] = (gh_ref[...].astype(F32) * slope).astype(BF)

    FIRST, SECOND = (ZH, X), (X, ZH)

    def place(h, al, be):
        return (off(X, be), off(ZH, al)) if h == 0 else (off(X, al), off(ZH, be))

    def half(h, a, b, cc):
        return gbuf.at[a * 4 + b, pl.ds(pl.multiple_of(cc * 128 + h * 64, 64), 64), :]

    def quarter_of(h, q, a, b, cc):
        return gbuf.at[a * 4 + b, pl.ds(pl.multiple_of(cc * 128 + h * 64 + q * 32, 32), 32), :]

    def slot(h, a, b, cc):
        return rg.at[h, a * 8 + b * 2 + cc]

    def qslot(h, q, a, b, cc):
        return (rh if q else rg).at[h, a * 8 + b * 2 + cc]

    def send(h, al, stage, sign):
        a, b = place(h, al, 0)
        ref = half(h, a, b, c)
        axis = (FIRST, SECOND)[stage][h]
        sem = sa.at[h, sign] if stage == 0 else sb.at[h, al * 4 + sign]
        return remote(ref, ref, sem, slot(h, a, b, c), {axis: off(axis, (1, 3)[sign])})

    def onward(h, al, stage, q):
        a, b = place(h, 3 - 2 * q, 0) if stage == 0 else place(h, al, 3 - 2 * q)
        ref = quarter_of(h, q, a, b, c)
        axis = (FIRST, SECOND)[stage][h]
        sem = sa.at[h, 2 + q] if stage == 0 else sb.at[h, al * 4 + 2 + q]
        return remote(ref, ref, sem, qslot(h, q, a, b, c), {axis: off(axis, (1, 3)[q])})

    def to_core(h, al, be):
        a, b = place(h, al, be)
        ref = half(h, a, b, c)
        return remote(ref, ref, sc.at[h, al * 4 + be], slot(h, a, b, c), {C: 1 - c})

    def arrive(h, al, be, dc):
        a, b = place(h, al, be)
        cc = off(C, dc)
        if dc == 0 and (be == 2 or (be == 0 and al == 2)):
            for q in (0, 1):
                ref = quarter_of(h, q, a, b, cc)
                remote(ref, ref, sa.at[0, 0], qslot(h, q, a, b, cc), {C: 1 - c}).wait_recv()
        else:
            ref = half(h, a, b, cc)
            remote(ref, ref, sa.at[0, 0], slot(h, a, b, cc), {C: 1 - c}).wait_recv()

    def process(al, be):
        for h in (1, 0):
            arrive(h, al, be, 0)
            if be == 0:
                if al != 2:
                    onward(h, al, 0, 1 if al == 1 else 0).start()
                for sign in (0, 1):
                    send(h, al, 1, sign).start()
            elif be != 2:
                onward(h, al, 1, 1 if be == 1 else 0).start()
            to_core(h, al, be).start()

    for h in (1, 0):
        for sign in (0, 1):
            send(h, 0, 0, sign).start()
    for h in (1, 0):
        for sign in (0, 1):
            send(h, 0, 1, sign).start()
    for h in (0, 1):
        to_core(h, 0, 0).start()
    for i in ((1, 1), (3, 1), (2, 0), (2, 1)):
        piece(*i).start()

    me = x * 8 + zh * 2 + c

    def find(ref, label):
        return lax.fori_loop(0, 32, lambda i, at: jnp.where(ref[0, i] == me, label(i), at), 0)

    whole_t = find(owner_ref, lambda i: i)
    split_t = find(sowner_ref, lambda i: 32 + i // CS)
    split_c = find(sowner_ref, lambda i: i // CS)
    wtct[:, :128] = w_v[whole_t].T
    wtct[:, 128:] = w_v[split_t].T
    load_keys.wait()
    keys_c[...] = lks_ref[split_c]

    def count_block(keys, out, cols):
        lo = jnp.bitwise_and(keys, 127)
        field = jnp.left_shift(1, jnp.right_shift(keys, 7) * 4)
        sub = lax.broadcasted_iota(jnp.int32, (128, 128), 0)
        packed = jnp.zeros((128, 128), jnp.int32)
        for p in range(8):
            packed += jnp.where(lo[p : p + 1, :] == sub, field[p : p + 1, :], 0)
        for h in range(8):
            n = jnp.bitwise_and(jnp.right_shift(packed, 4 * h), 15)
            out[h * 128 : h * 128 + 128, cols] = n.astype(F32).astype(BF)

    def count(k, carry=None):
        cols = pl.ds(pl.multiple_of(k * 128, 128), 128)
        count_block(lkw_ref[:, cols], cw, cols)
        count_block(keys_c[:, cols], cs, cols)

    steps = [(1, 0), (3, 0), (0, 1), (0, 3), (2, 0), (0, 2)]
    for i, (al, be) in enumerate(steps):
        pl.loop(i * 5, i * 5 + 5)(lambda k: count(k))
        process(al, be)

    pl.loop(30, 32)(lambda k: count(k))

    own_piece.wait()
    for i in range(1, 8):
        piece_in(off(X, i // 2), off(C, i % 2)).wait_recv()
    for d in range(4):
        arrive(0, 0, d, 1)
        arrive(1, d, 0, 1)

    def along_y(d, q):
        yd = off(Y, d)
        return remote(pp.at[yd, q], yr.at[y, q], sy.at[d - 1, q], ry.at[y, q], {Y: yd})

    def from_y(d, q):
        ys = off(Y, d)
        return remote(pp.at[ys, q], yr.at[ys, q], sy.at[0, q], ry.at[ys, q], {Y: ys})

    def bias_y(d):
        return remote(bs, by.at[y], sby.at[d - 1], rby.at[y], {Y: off(Y, d)})

    def bias_from_y(d):
        ys = off(Y, d)
        return remote(bs, by.at[ys], sby.at[0], rby.at[ys], {Y: ys})

    for dz in (1, 3, 2, 0):
        q = off(ZH, dz)
        total = jnp.zeros((160, 512), F32)
        for xs in range(4):
            both = jnp.concatenate([pr[2 * xs, q], pr[2 * xs + 1, q]], axis=1)
            total += jnp.dot(both, gbuf[xs * 4 + zh], preferred_element_type=F32)
        low = total.astype(BF)
        for j in range(4):
            pp[j, q] = low[:, 128 * j : 128 * j + 128]
        for d in (1, 3, 2):
            along_y(d, q).start()

    col = jnp.zeros((8, 512), F32)
    for xs in range(4):
        col += jnp.dot(jnp.ones((8, 256), BF), gbuf[xs * 4 + zh], preferred_element_type=F32)
    bs[...] = jnp.zeros_like(bs)
    for j in range(4):
        bs[j : j + 1, :] = col[0:1, 128 * j : 128 * j + 128]
    for d in (1, 3, 2):
        bias_y(d).start()

    accw[...] = jnp.zeros_like(accw)
    accs[...] = jnp.zeros_like(accs)

    def tables(da, db):
        cb = off(X, da) * 4 + off(ZH, db)
        rows = gbuf[cb]
        cols = pl.ds(pl.multiple_of(cb * 256, 256), 256)
        back = jnp.dot(rows, wtct[...], preferred_element_type=F32).astype(BF)
        accw[...] += jnp.dot(cw[:, cols], back[:, :128], preferred_element_type=F32)
        accs[...] += jnp.dot(cs[:, cols], back[:, 128:], preferred_element_type=F32)

    def other_core(da, db):
        if db:
            arrive(0, db, da, 1)
            arrive(1, da, db, 1)

    process(1, 1)
    tables(0, 0)
    process(1, 3)
    tables(1, 0)
    process(3, 1)
    tables(3, 0)
    process(3, 3)
    tables(2, 0)
    process(2, 1)
    other_core(0, 1)
    tables(0, 1)
    process(2, 3)
    other_core(0, 3)
    tables(0, 3)

    zme = zh * 2 + zl
    others = [(1, 0), (1, 1), (3, 0), (3, 1), (2, 0), (2, 1), (0, 1)]

    def along_z(i):
        zd, ld = off(ZH, others[i][0]), off(ZL, others[i][1])
        return remote(zs.at[zd * 2 + ld], zr.at[zme], sz.at[i], rz.at[zme], {ZH: zd, ZL: ld})

    def from_z(i):
        s = off(ZH, others[i][0]) * 2 + off(ZL, others[i][1])
        return remote(zs.at[s], zr.at[s], sz.at[0], rz.at[s], {C: 1 - c})

    def bias_z(i):
        zd, ld = off(ZH, others[i][0]), off(ZL, others[i][1])
        return remote(bt, bz.at[zme], sbz.at[i], rbz.at[zme], {ZH: zd, ZL: ld})

    def bias_from_z(i):
        s = off(ZH, others[i][0]) * 2 + off(ZL, others[i][1])
        return remote(bt, bz.at[s], sbz.at[0], rbz.at[s], {C: 1 - c})

    for dz in (1, 3, 2, 0):
        q = off(ZH, dz)
        for d in (1, 3, 2):
            from_y(d, q).wait_recv()
        total = pp[y, q].astype(F32)
        for d in (1, 2, 3):
            total += yr[off(Y, d), q].astype(F32)
        zs[q * 2] = total[:80].astype(BF)
        zs[q * 2 + 1] = total[80:].astype(BF)
        for i in range(7):
            if others[i][0] == dz:
                along_z(i).start()

    for d in (1, 3, 2):
        bias_from_y(d).wait_recv()
    col = bs[...]
    for d in (1, 2, 3):
        col += by[off(Y, d)]
    bt[...] = col
    for i in range(7):
        bias_z(i).start()

    process(1, 2)
    other_core(0, 2)
    tables(0, 2)
    process(3, 2)
    for da, db in ((1, 1), (1, 3), (3, 1)):
        other_core(da, db)
        tables(da, db)
    process(2, 2)

    for i in range(7):
        from_z(i).wait_recv()
    total = zs[zme].astype(F32)
    for i in range(7):
        total += zr[off(ZH, others[i][0]) * 2 + off(ZL, others[i][1])].astype(F32)

    gme = y * 2 + zl
    gr[gme] = total.astype(BF)
    group = [(1, 0), (3, 0), (0, 1), (1, 1), (3, 1), (2, 0), (2, 1)]

    def give(i):
        yd, ld = off(Y, group[i][0]), off(ZL, group[i][1])
        return remote(gr.at[gme], gr.at[gme], sg.at[i], rgf.at[gme], {Y: yd, ZL: ld})

    def take(i):
        g = off(Y, group[i][0]) * 2 + off(ZL, group[i][1])
        return remote(gr.at[g], gr.at[g], sg.at[0], rgf.at[g], {C: 1 - c})

    for i in range(7):
        give(i).start()

    for da, db in ((3, 3), (2, 1), (1, 2), (2, 3), (3, 2), (2, 2)):
        other_core(da, db)
        tables(da, db)

    for i in range(7):
        bias_from_z(i).wait_recv()
    col = bt[...]
    for i in range(7):
        col += bz[off(ZH, others[i][0]) * 2 + off(ZL, others[i][1])]
    for j in range(4):
        gb_ref[0:1, 128 * j : 128 * j + 128] = col[j : j + 1, :]

    for i in range(7):
        take(i).wait_recv()
    for yy in range(4):
        for ll in range(2):
            gf_ref[80 * ll : 80 * ll + 80, 128 * yy : 128 * yy + 128] = gr[yy * 2 + ll].astype(F32)
    for i in range(1, 8):
        piece(i // 2, i % 2).wait_send()
    for h in (0, 1):
        for sign in (0, 1):
            send(h, 0, 0, sign).wait_send()
            onward(h, 0, 0, sign).wait_send()
        for al in range(4):
            for sign in (0, 1):
                send(h, al, 1, sign).wait_send()
                onward(h, al, 1, sign).wait_send()
            for be in range(4):
                to_core(h, al, be).wait_send()

    for d in (1, 2, 3):
        for q in range(4):
            along_y(d, q).wait_send()
        bias_y(d).wait_send()
    for i in range(7):
        along_z(i).wait_send()
        bias_z(i).wait_send()
        give(i).wait_send()


def update(
    sowner_ref, gfi_ref, gbi_ref, gw_ref, gs_ref, tw_ref, aw_ref, ts_ref, as_ref,
    gf_ref, gb_ref, nw_ref, ns_ref,
):
    me = lax.axis_index(X) * 8 + lax.axis_index(ZH) * 2 + lax.axis_index(C)
    shard = lax.fori_loop(0, 32, lambda i, at: jnp.where(sowner_ref[0, i] == me, i, at), 0)
    split_c = lax.div(shard, CS)
    quarter = lax.rem(shard, CS)
    gf_ref[...] = gfi_ref[...]
    gb_ref[...] = gbi_ref[...]
    grad = gw_ref[...].T
    square = jnp.sum(grad * grad, axis=0, keepdims=True)
    scale = LEARN_RATE / (jnp.sqrt(aw_ref[...] + square / E) + EPSILON)
    nw_ref[...] = tw_ref[...] - grad * scale
    grads = gs_ref[...].T
    squares = jnp.sum(grads * grads, axis=0, keepdims=True)
    tab = lax.broadcasted_iota(jnp.int32, (8, 1024), 0)
    state = jnp.sum(jnp.where(tab == split_c, as_ref[...], 0.0), axis=0, keepdims=True)
    scales = LEARN_RATE / (jnp.sqrt(state + squares / E) + EPSILON)
    mine = grads[:COLS]
    for q in range(1, CS):
        mine = jnp.where(quarter == q, grads[q * COLS : (q + 1) * COLS], mine)
    ns_ref[...] = ts_ref[...] - mine * scales


VM = pl.BlockSpec(memory_space=pltpu.VMEM)
SM = pl.BlockSpec(memory_space=pltpu.SMEM)
ANY = pl.BlockSpec(memory_space=pl.ANY)
DMA = pltpu.SemaphoreType.DMA


def per_device(
    pooled, grad_hidden, w_first, bias_first, table_owner, shard_owner, lookups_whole,
    lookups_split, table_whole, accum_whole, table_split, accum_split,
):
    keys_whole = jnp.swapaxes(lookups_whole[0, 0], 0, 1)
    keys_split = jnp.swapaxes(lookups_split[0], 1, 2)
    grad_first, grad_bias, grad_whole, grad_split = pl.pallas_call(
        kernel,
        out_shape=(
            jax.ShapeDtypeStruct((160, 512), F32),
            jax.ShapeDtypeStruct((1, 512), F32),
            jax.ShapeDtypeStruct((1024, 128), F32),
            jax.ShapeDtypeStruct((1024, 128), F32),
        ),
        in_specs=[SM, SM, VM, VM, ANY, VM, VM, ANY],
        out_specs=(VM, VM, VM, VM),
        scratch_shapes=[
            pltpu.VMEM((40, 128, 512), BF),
            pltpu.VMEM((8, 8, 4096), jnp.int32),
            pltpu.VMEM((4, 2, 4, 160, 128), BF),
            pltpu.VMEM((8, 4, 160, 128), BF),
            pltpu.VMEM((16, 256, 512), BF),
            pltpu.VMEM((4, 4, 160, 128), BF),
            pltpu.VMEM((4, 4, 160, 128), BF),
            pltpu.VMEM((8, 80, 128), BF),
            pltpu.VMEM((8, 80, 128), BF),
            pltpu.VMEM((8, 128), F32),
            pltpu.VMEM((4, 8, 128), F32),
            pltpu.VMEM((8, 128), F32),
            pltpu.VMEM((8, 8, 128), F32),
            pltpu.VMEM((1024, 4096), BF),
            pltpu.VMEM((1024, 4096), BF),
            pltpu.VMEM((512, 256), BF),
            pltpu.VMEM((128, 512), F32),
            pltpu.VMEM((8, 4096), jnp.int32),
            pltpu.VMEM((8, 80, 128), BF),
            DMA,
            DMA,
            DMA,
            DMA((8,)), DMA((8,)),
            DMA((2, 4)), DMA((2, 16)), DMA((2, 16)), DMA((2, 32)), DMA((2, 32)),
            DMA((3, 4)), DMA((4, 4)),
            DMA((7,)), DMA((8,)),
            DMA((7,)), DMA((8,)),
            DMA((3,)), DMA((4,)),
            DMA((7,)), DMA((8,)),
        ],
        compiler_params=pltpu.CompilerParams(
            collective_id=0, has_side_effects=True, vmem_limit_bytes=58 * 2**20
        ),
        name="step",
    )(
        table_owner, shard_owner, pooled, grad_hidden, w_first.reshape(40, 128, 512), bias_first[None],
        keys_whole, keys_split,
    )
    grad_first, grad_bias, new_whole, new_split = pl.pallas_call(
        update,
        out_shape=(
            jax.ShapeDtypeStruct((160, 512), F32),
            jax.ShapeDtypeStruct((1, 512), F32),
            jax.ShapeDtypeStruct((128, 1024), F32),
            jax.ShapeDtypeStruct((32, 1024), F32),
        ),
        in_specs=[SM, VM, VM, VM, VM, VM, VM, VM, VM],
        out_specs=(VM, VM, VM, VM),
        name="update",
    )(
        shard_owner, grad_first, grad_bias, grad_whole, grad_split,
        table_whole[0, 0], accum_whole[0], table_split[0, 0], accum_split[0],
    )
    return grad_first, grad_bias[0], new_whole[None, None], new_split[None, None]


def solution(mesh):
    finer = Mesh(mesh.devices.reshape(2, 4, 4, 4, 2), GRP_MEM)
    in_specs = (
        P(GRP_MEM, None),
        P(GRP_MEM, None),
        P(),
        P(),
        P(GRP, None),
        P(GRP, None),
        P(GRP, MEM, None, None),
        P(GRP, None, None, None),
        P(GRP, MEM, None, None),
        P(GRP, MEM, None),
        P(GRP, MEM, None, None),
        P(GRP, None, None),
    )
    out_specs = (P(MEM, None), P(), P(GRP, MEM, None, None), P(GRP, MEM, None, None))
    return jax.shard_map(
        per_device, mesh=finer, in_specs=in_specs, out_specs=out_specs, check_vma=False
    )
```

```python
import jax
import jax.numpy as jnp
from jax import lax
from jax.experimental import pallas as pl
from jax.experimental.pallas import tpu as pltpu
from jax.sharding import Mesh
from jax.sharding import PartitionSpec as P

E = 128
CS = 4
NEAR = 96
COLS = 32
ZL, Y, X, ZH, C = "grp_0", "grp_1", "mem_0", "mem_1", "mem_2"
SIZE = {ZL: 2, Y: 4, X: 4, ZH: 4, C: 2}
MEM = (X, ZH, C)
GRP = (ZL, Y)
GRP_MEM = GRP + MEM
LEARN_RATE = 0.5
EPSILON = 1e-08
MESH = pl.DeviceIdType.MESH
BF = jnp.bfloat16
F32 = jnp.float32


def remote(src, dst, ssem, rsem, dev):
    return pltpu.make_async_remote_copy(
        src_ref=src, dst_ref=dst, send_sem=ssem, recv_sem=rsem, device_id=dev, device_id_type=MESH
    )


def kernel(
    owner_ref, sowner_ref, pooled_ref, gh_ref, w_hbm, bias_ref, lkw_ref, lks_hbm,
    gf_ref, gb_ref, accw, accs,
    w_v, lks_ref, pt, pr, gbuf, pp, yr, zs, zr, bs, by, bt, bz, cw, cs, wtct, pre, keys_c, gr,
    w_sem, lk_sem, own_sem, sp, rp, sa, sb, sc, rg, rh, sy, ry, sz, rz, sg, rgf, sby, rby, sbz, rbz,
):
    x, zh, c = lax.axis_index(X), lax.axis_index(ZH), lax.axis_index(C)
    y, zl = lax.axis_index(Y), lax.axis_index(ZL)

    def off(axis, d):
        return lax.rem(lax.axis_index(axis) + d, SIZE[axis])

    load_w = pltpu.make_async_copy(w_hbm, w_v, w_sem)
    load_w.start()
    load_keys = pltpu.make_async_copy(lks_hbm, lks_ref, lk_sem)
    load_keys.start()

    barrier = pltpu.get_barrier_semaphore()
    peers = []
    for d in (1, 2, 3):
        peers.append({X: off(X, d)})
        peers.append({X: off(X, d), C: 1 - c})
        peers.append({ZH: off(ZH, d)})
        peers.append({ZH: off(ZH, d), ZL: 1 - zl})
        peers.append({Y: off(Y, d)})
        peers.append({Y: off(Y, d), ZL: 1 - zl})
    peers.append({C: 1 - c})
    peers.append({ZL: 1 - zl})
    for p in peers:
        pl.semaphore_signal(barrier, inc=1, device_id=p, device_id_type=MESH)

    for t in range(40):
        tile = pooled_ref[:, 128 * t : 128 * t + 128].T
        done = 0
        while done < 128:
            f = 128 * t + done
            m, r = f // 160, f % 160
            n = min(160 - r, 128 - done)
            pt[(m // 8), m % 2, (m // 2) % 4, r : r + n, :] = tile[done : done + n, :]
            done += n

    def piece(dx, dc):
        xd, cd = off(X, dx), off(C, dc)
        i = dx * 2 + dc
        return remote(pt.at[xd, cd], pr.at[x * 2 + c], sp.at[i], rp.at[x * 2 + c], {X: xd, C: cd})

    def piece_in(xs, csrc):
        return remote(pt.at[0, 0], pr.at[xs * 2 + csrc], sp.at[0], rp.at[xs * 2 + csrc], {C: 1 - c})

    own_piece = pltpu.make_async_copy(pt.at[x, c], pr.at[x * 2 + c], own_sem)
    load_w.wait()
    pre[...] = jnp.zeros_like(pre)

    def tower(k):
        cols = pl.ds(pl.multiple_of(k * 640, 640), 640)
        wk = w_v[pl.ds(k * 5, 5)].reshape(640, 512)
        pre[...] += jnp.dot(pooled_ref[:, cols], wk, preferred_element_type=F32)

    pl.loop(0, 3)(tower)
    pl.semaphore_wait(barrier, len(peers))
    piece(1, 0).start()
    piece(3, 0).start()
    piece(0, 1).start()
    own_piece.start()
    pl.loop(3, 8)(tower)

    pre_act = pre[...] + bias_ref[...]
    sg_ = jax.nn.sigmoid(pre_act)
    slope = sg_ * (1.0 + pre_act * (1.0 - sg_))
    my_rows = pl.ds(pl.multiple_of(c * 128, 128), 128)
    gbuf[x * 4 + zh, my_rows, :] = (gh_ref[...].astype(F32) * slope).astype(BF)

    FIRST, SECOND = (ZH, X), (X, ZH)

    def place(h, al, be):
        return (off(X, be), off(ZH, al)) if h == 0 else (off(X, al), off(ZH, be))

    def half(h, a, b, cc):
        start, rows = ((0, NEAR), (NEAR, 128 - NEAR))[h]
        return gbuf.at[a * 4 + b, pl.ds(pl.multiple_of(cc * 128 + start, 16), rows), :]

    def quarter_of(h, q, a, b, cc):
        start, rows = ((0, NEAR // 2), (NEAR, 64 - NEAR // 2))[h]
        return gbuf.at[a * 4 + b, pl.ds(pl.multiple_of(cc * 128 + start + q * rows, 16), rows), :]

    def slot(h, a, b, cc):
        return rg.at[h, a * 8 + b * 2 + cc]

    def qslot(h, q, a, b, cc):
        return (rh if q else rg).at[h, a * 8 + b * 2 + cc]

    def send(h, al, stage, sign):
        a, b = place(h, al, 0)
        ref = half(h, a, b, c)
        axis = (FIRST, SECOND)[stage][h]
        sem = sa.at[h, sign] if stage == 0 else sb.at[h, al * 4 + sign]
        return remote(ref, ref, sem, slot(h, a, b, c), {axis: off(axis, (1, 3)[sign])})

    def onward(h, al, stage, q):
        a, b = place(h, 3 - 2 * q, 0) if stage == 0 else place(h, al, 3 - 2 * q)
        ref = quarter_of(h, q, a, b, c)
        axis = (FIRST, SECOND)[stage][h]
        sem = sa.at[h, 2 + q] if stage == 0 else sb.at[h, al * 4 + 2 + q]
        return remote(ref, ref, sem, qslot(h, q, a, b, c), {axis: off(axis, (1, 3)[q])})

    def to_core(h, al, be):
        a, b = place(h, al, be)
        ref = half(h, a, b, c)
        return remote(ref, ref, sc.at[h, al * 4 + be], slot(h, a, b, c), {C: 1 - c})

    def arrive(h, al, be, dc):
        a, b = place(h, al, be)
        cc = off(C, dc)
        if dc == 0 and (be == 2 or (be == 0 and al == 2)):
            for q in (0, 1):
                ref = quarter_of(h, q, a, b, cc)
                remote(ref, ref, sa.at[0, 0], qslot(h, q, a, b, cc), {C: 1 - c}).wait_recv()
        else:
            ref = half(h, a, b, cc)
            remote(ref, ref, sa.at[0, 0], slot(h, a, b, cc), {C: 1 - c}).wait_recv()

    def process(*steps):
        for h, al, be in steps:
            arrive(h, al, be, 0)
            if be == 0:
                if al != 2:
                    onward(h, al, 0, 1 if al == 1 else 0).start()
                for sign in (0, 1):
                    send(h, al, 1, sign).start()
            elif be != 2:
                onward(h, al, 1, 1 if be == 1 else 0).start()
            to_core(h, al, be).start()

    for h in (1, 0):
        for sign in (0, 1):
            send(h, 0, 0, sign).start()
    for h in (1, 0):
        for sign in (0, 1):
            send(h, 0, 1, sign).start()
    for h in (0, 1):
        to_core(h, 0, 0).start()
    for i in ((1, 1), (3, 1), (2, 0), (2, 1)):
        piece(*i).start()

    me = x * 8 + zh * 2 + c

    def find(ref, label):
        return lax.fori_loop(0, 32, lambda i, at: jnp.where(ref[0, i] == me, label(i), at), 0)

    whole_t = find(owner_ref, lambda i: i)
    split_t = find(sowner_ref, lambda i: 32 + i // CS)
    split_c = find(sowner_ref, lambda i: i // CS)
    wtct[:, :128] = w_v[whole_t].T
    wtct[:, 128:] = w_v[split_t].T
    load_keys.wait()
    keys_c[...] = lks_ref[split_c]

    def count_block(keys, out, cols):
        lo = jnp.bitwise_and(keys, 127)
        field = jnp.left_shift(1, jnp.right_shift(keys, 7) * 4)
        sub = lax.broadcasted_iota(jnp.int32, (128, 128), 0)
        packed = jnp.zeros((128, 128), jnp.int32)
        for p in range(8):
            packed += jnp.where(lo[p : p + 1, :] == sub, field[p : p + 1, :], 0)
        for h in range(8):
            n = jnp.bitwise_and(jnp.right_shift(packed, 4 * h), 15)
            out[h * 128 : h * 128 + 128, cols] = n.astype(F32).astype(BF)

    def count(k, carry=None):
        cols = pl.ds(pl.multiple_of(k * 128, 128), 128)
        count_block(lkw_ref[:, cols], cw, cols)
        count_block(keys_c[:, cols], cs, cols)

    steps = [
        (1, 1, 0), (0, 0, 1), (1, 3, 0), (0, 0, 3), (0, 1, 0), (1, 0, 1), (0, 3, 0), (1, 0, 3),
        (0, 2, 0), (1, 0, 2), (1, 1, 1), (1, 1, 3), (1, 3, 1), (1, 3, 3), (1, 1, 2), (1, 3, 2),
    ]
    for i, step in enumerate(steps):
        pl.loop(i * 2, i * 2 + 2)(lambda k: count(k))
        process(step)

    process((1, 2, 0), (0, 0, 2))

    own_piece.wait()
    for i in range(1, 8):
        piece_in(off(X, i // 2), off(C, i % 2)).wait_recv()
    for d in range(4):
        arrive(0, 0, d, 1)
        arrive(1, d, 0, 1)

    def along_y(d, q):
        yd = off(Y, d)
        return remote(pp.at[yd, q], yr.at[y, q], sy.at[d - 1, q], ry.at[y, q], {Y: yd})

    def from_y(d, q):
        ys = off(Y, d)
        return remote(pp.at[ys, q], yr.at[ys, q], sy.at[0, q], ry.at[ys, q], {Y: ys})

    def bias_y(d):
        return remote(bs, by.at[y], sby.at[d - 1], rby.at[y], {Y: off(Y, d)})

    def bias_from_y(d):
        ys = off(Y, d)
        return remote(bs, by.at[ys], sby.at[0], rby.at[ys], {Y: ys})

    for dz in (1, 3, 2, 0):
        q = off(ZH, dz)
        total = jnp.zeros((160, 512), F32)
        for xs in range(4):
            both = jnp.concatenate([pr[2 * xs, q], pr[2 * xs + 1, q]], axis=1)
            total += jnp.dot(both, gbuf[xs * 4 + zh], preferred_element_type=F32)
        low = total.astype(BF)
        for j in range(4):
            pp[j, q] = low[:, 128 * j : 128 * j + 128]
        for d in (1, 3, 2):
            along_y(d, q).start()

    col = jnp.zeros((8, 512), F32)
    for xs in range(4):
        col += jnp.dot(jnp.ones((8, 256), BF), gbuf[xs * 4 + zh], preferred_element_type=F32)
    bs[...] = jnp.zeros_like(bs)
    for j in range(4):
        bs[j : j + 1, :] = col[0:1, 128 * j : 128 * j + 128]
    for d in (1, 3, 2):
        bias_y(d).start()

    accw[...] = jnp.zeros_like(accw)
    accs[...] = jnp.zeros_like(accs)

    def tables(da, db):
        cb = off(X, da) * 4 + off(ZH, db)
        rows = gbuf[cb]
        cols = pl.ds(pl.multiple_of(cb * 256, 256), 256)
        back = jnp.dot(rows, wtct[...], preferred_element_type=F32).astype(BF)
        accw[...] += jnp.dot(cw[:, cols], back[:, :128], preferred_element_type=F32)
        accs[...] += jnp.dot(cs[:, cols], back[:, 128:], preferred_element_type=F32)

    def other_core(da, db):
        if db:
            arrive(0, db, da, 1)
            arrive(1, da, db, 1)

    process((0, 1, 1))
    tables(0, 0)
    process((0, 3, 1))
    tables(1, 0)
    process((1, 2, 1))
    tables(3, 0)
    process((0, 1, 3))
    tables(2, 0)
    process((0, 3, 3))
    other_core(0, 1)
    tables(0, 1)
    process((1, 2, 3))
    other_core(0, 3)
    tables(0, 3)
    process((0, 2, 1))
    other_core(0, 2)
    tables(0, 2)
    process((0, 2, 3))

    zme = zh * 2 + zl
    others = [(1, 0), (1, 1), (3, 0), (3, 1), (2, 0), (2, 1), (0, 1)]

    def along_z(i):
        zd, ld = off(ZH, others[i][0]), off(ZL, others[i][1])
        return remote(zs.at[zd * 2 + ld], zr.at[zme], sz.at[i], rz.at[zme], {ZH: zd, ZL: ld})

    def from_z(i):
        s = off(ZH, others[i][0]) * 2 + off(ZL, others[i][1])
        return remote(zs.at[s], zr.at[s], sz.at[0], rz.at[s], {C: 1 - c})

    def bias_z(i):
        zd, ld = off(ZH, others[i][0]), off(ZL, others[i][1])
        return remote(bt, bz.at[zme], sbz.at[i], rbz.at[zme], {ZH: zd, ZL: ld})

    def bias_from_z(i):
        s = off(ZH, others[i][0]) * 2 + off(ZL, others[i][1])
        return remote(bt, bz.at[s], sbz.at[0], rbz.at[s], {C: 1 - c})

    for dz in (1, 3, 2, 0):
        q = off(ZH, dz)
        for d in (1, 3, 2):
            from_y(d, q).wait_recv()
        total = pp[y, q].astype(F32)
        for d in (1, 2, 3):
            total += yr[off(Y, d), q].astype(F32)
        zs[q * 2] = total[:80].astype(BF)
        zs[q * 2 + 1] = total[80:].astype(BF)
        for i in range(7):
            if others[i][0] == dz:
                along_z(i).start()

    for d in (1, 3, 2):
        bias_from_y(d).wait_recv()
    col = bs[...]
    for d in (1, 2, 3):
        col += by[off(Y, d)]
    bt[...] = col
    for i in range(7):
        bias_z(i).start()

    process((0, 1, 2))
    other_core(1, 1)
    tables(1, 1)
    process((0, 3, 2))
    other_core(1, 3)
    tables(1, 3)
    process((1, 2, 2), (0, 2, 2))
    other_core(3, 1)
    tables(3, 1)

    for i in range(7):
        from_z(i).wait_recv()
    total = zs[zme].astype(F32)
    for i in range(7):
        total += zr[off(ZH, others[i][0]) * 2 + off(ZL, others[i][1])].astype(F32)

    gme = y * 2 + zl
    gr[gme] = total.astype(BF)
    group = [(1, 0), (3, 0), (0, 1), (1, 1), (3, 1), (2, 0), (2, 1)]

    def give(i):
        yd, ld = off(Y, group[i][0]), off(ZL, group[i][1])
        return remote(gr.at[gme], gr.at[gme], sg.at[i], rgf.at[gme], {Y: yd, ZL: ld})

    def take(i):
        g = off(Y, group[i][0]) * 2 + off(ZL, group[i][1])
        return remote(gr.at[g], gr.at[g], sg.at[0], rgf.at[g], {C: 1 - c})

    for i in range(7):
        give(i).start()

    for da, db in ((3, 3), (2, 1), (1, 2), (2, 3), (3, 2), (2, 2)):
        other_core(da, db)
        tables(da, db)

    for i in range(7):
        bias_from_z(i).wait_recv()
    col = bt[...]
    for i in range(7):
        col += bz[off(ZH, others[i][0]) * 2 + off(ZL, others[i][1])]
    for j in range(4):
        gb_ref[0:1, 128 * j : 128 * j + 128] = col[j : j + 1, :]

    for i in range(7):
        take(i).wait_recv()
    for yy in range(4):
        for ll in range(2):
            gf_ref[80 * ll : 80 * ll + 80, 128 * yy : 128 * yy + 128] = gr[yy * 2 + ll].astype(F32)
    for i in range(1, 8):
        piece(i // 2, i % 2).wait_send()
    for h in (0, 1):
        for sign in (0, 1):
            send(h, 0, 0, sign).wait_send()
            onward(h, 0, 0, sign).wait_send()
        for al in range(4):
            for sign in (0, 1):
                send(h, al, 1, sign).wait_send()
                onward(h, al, 1, sign).wait_send()
            for be in range(4):
                to_core(h, al, be).wait_send()

    for d in (1, 2, 3):
        for q in range(4):
            along_y(d, q).wait_send()
        bias_y(d).wait_send()
    for i in range(7):
        along_z(i).wait_send()
        bias_z(i).wait_send()
        give(i).wait_send()


def update(
    sowner_ref, gfi_ref, gbi_ref, gw_ref, gs_ref, tw_ref, aw_ref, ts_ref, as_ref,
    gf_ref, gb_ref, nw_ref, ns_ref,
):
    me = lax.axis_index(X) * 8 + lax.axis_index(ZH) * 2 + lax.axis_index(C)
    shard = lax.fori_loop(0, 32, lambda i, at: jnp.where(sowner_ref[0, i] == me, i, at), 0)
    split_c = lax.div(shard, CS)
    quarter = lax.rem(shard, CS)
    gf_ref[...] = gfi_ref[...]
    gb_ref[...] = gbi_ref[...]
    grad = gw_ref[...].T
    square = jnp.sum(grad * grad, axis=0, keepdims=True)
    scale = LEARN_RATE / (jnp.sqrt(aw_ref[...] + square / E) + EPSILON)
    nw_ref[...] = tw_ref[...] - grad * scale
    grads = gs_ref[...].T
    squares = jnp.sum(grads * grads, axis=0, keepdims=True)
    tab = lax.broadcasted_iota(jnp.int32, (8, 1024), 0)
    state = jnp.sum(jnp.where(tab == split_c, as_ref[...], 0.0), axis=0, keepdims=True)
    scales = LEARN_RATE / (jnp.sqrt(state + squares / E) + EPSILON)
    mine = grads[:COLS]
    for q in range(1, CS):
        mine = jnp.where(quarter == q, grads[q * COLS : (q + 1) * COLS], mine)
    ns_ref[...] = ts_ref[...] - mine * scales


VM = pl.BlockSpec(memory_space=pltpu.VMEM)
SM = pl.BlockSpec(memory_space=pltpu.SMEM)
ANY = pl.BlockSpec(memory_space=pl.ANY)
DMA = pltpu.SemaphoreType.DMA


def per_device(
    pooled, grad_hidden, w_first, bias_first, table_owner, shard_owner, lookups_whole,
    lookups_split, table_whole, accum_whole, table_split, accum_split,
):
    keys_whole = jnp.swapaxes(lookups_whole[0, 0], 0, 1)
    keys_split = jnp.swapaxes(lookups_split[0], 1, 2)
    grad_first, grad_bias, grad_whole, grad_split = pl.pallas_call(
        kernel,
        out_shape=(
            jax.ShapeDtypeStruct((160, 512), F32),
            jax.ShapeDtypeStruct((1, 512), F32),
            jax.ShapeDtypeStruct((1024, 128), F32),
            jax.ShapeDtypeStruct((1024, 128), F32),
        ),
        in_specs=[SM, SM, VM, VM, ANY, VM, VM, ANY],
        out_specs=(VM, VM, VM, VM),
        scratch_shapes=[
            pltpu.VMEM((40, 128, 512), BF),
            pltpu.VMEM((8, 8, 4096), jnp.int32),
            pltpu.VMEM((4, 2, 4, 160, 128), BF),
            pltpu.VMEM((8, 4, 160, 128), BF),
            pltpu.VMEM((16, 256, 512), BF),
            pltpu.VMEM((4, 4, 160, 128), BF),
            pltpu.VMEM((4, 4, 160, 128), BF),
            pltpu.VMEM((8, 80, 128), BF),
            pltpu.VMEM((8, 80, 128), BF),
            pltpu.VMEM((8, 128), F32),
            pltpu.VMEM((4, 8, 128), F32),
            pltpu.VMEM((8, 128), F32),
            pltpu.VMEM((8, 8, 128), F32),
            pltpu.VMEM((1024, 4096), BF),
            pltpu.VMEM((1024, 4096), BF),
            pltpu.VMEM((512, 256), BF),
            pltpu.VMEM((128, 512), F32),
            pltpu.VMEM((8, 4096), jnp.int32),
            pltpu.VMEM((8, 80, 128), BF),
            DMA,
            DMA,
            DMA,
            DMA((8,)), DMA((8,)),
            DMA((2, 4)), DMA((2, 16)), DMA((2, 16)), DMA((2, 32)), DMA((2, 32)),
            DMA((3, 4)), DMA((4, 4)),
            DMA((7,)), DMA((8,)),
            DMA((7,)), DMA((8,)),
            DMA((3,)), DMA((4,)),
            DMA((7,)), DMA((8,)),
        ],
        compiler_params=pltpu.CompilerParams(
            collective_id=0, has_side_effects=True, vmem_limit_bytes=58 * 2**20
        ),
        name="step",
    )(
        table_owner, shard_owner, pooled, grad_hidden, w_first.reshape(40, 128, 512), bias_first[None],
        keys_whole, keys_split,
    )
    grad_first, grad_bias, new_whole, new_split = pl.pallas_call(
        update,
        out_shape=(
            jax.ShapeDtypeStruct((160, 512), F32),
            jax.ShapeDtypeStruct((1, 512), F32),
            jax.ShapeDtypeStruct((128, 1024), F32),
            jax.ShapeDtypeStruct((32, 1024), F32),
        ),
        in_specs=[SM, VM, VM, VM, VM, VM, VM, VM, VM],
        out_specs=(VM, VM, VM, VM),
        name="update",
    )(
        shard_owner, grad_first, grad_bias, grad_whole, grad_split,
        table_whole[0, 0], accum_whole[0], table_split[0, 0], accum_split[0],
    )
    return grad_first, grad_bias[0], new_whole[None, None], new_split[None, None]


def solution(mesh):
    finer = Mesh(mesh.devices.reshape(2, 4, 4, 4, 2), GRP_MEM)
    in_specs = (
        P(GRP_MEM, None),
        P(GRP_MEM, None),
        P(),
        P(),
        P(GRP, None),
        P(GRP, None),
        P(GRP, MEM, None, None),
        P(GRP, None, None, None),
        P(GRP, MEM, None, None),
        P(GRP, MEM, None),
        P(GRP, MEM, None, None),
        P(GRP, None, None),
    )
    out_specs = (P(MEM, None), P(), P(GRP, MEM, None, None), P(GRP, MEM, None, None))
    return jax.shard_map(
        per_device, mesh=finer, in_specs=in_specs, out_specs=out_specs, check_vma=False
    )
```
